32 devices in a mesh: src: 8 (over z, y), space: 4 (over x, core).
Axes of the slice: x: 2, y: 2, z: 4, core: 2. Of those that a mesh axis runs over, the one named last changes fastest.
Arguments:
- wavefield: float32 [8, 9, 32, 64, 128], P('src', None, 'space'), may hold values from -6 to 6
- strain_bank: bfloat16 [8, 6, 32, 64, 128], P('src', None, 'space'), may hold values from -6 to 6
- owners: int32 [4], replicated, may hold values from 0 to 7, as said below
- region: int32 [32, 64, 128], P('space'), may hold values from 0 to 7
- region_lambda: float32 [8], replicated, may hold values from 1 to 2
- region_mu: float32 [8], replicated, may hold values from 0.5 to 1
- region_buoyancy: float32 [8], replicated, may hold values from 0.5 to 1
Outputs:
- new_wavefield: float32 [8, 9, 32, 64, 128], P('src', None, 'space')
- lambda_kernel: float32 [32, 64, 128], P('space', 'src')
- mu_kernel: float32 [32, 64, 128], P('space', 'src')
The draws below stay inside these ranges and needn't reach their ends.
Inputs may be any that keep to these rules, and one draw needn't show every extreme that they name: `owners`: 4 distinct owner indices in an order drawn per run; 0 and 7 are always among them.
All inputs are finite; a program needn't handle non-finite values.
Results may differ from the reference program's by a relative error of at most 0.0003.
Values may be sent and summed in bfloat16 or wider, within the bound.
A program may use at most 128 MiB of HBM per device.

```python
import jax
import jax.numpy as jnp
from jax import lax

NY = 64
NZ = 128
STEPS = 4
REGIONS = 8
SOURCES = 8
OWNERS = 8
NX = 32


def draw_owners(key, part):
    first_key, second_key = jax.random.split(jax.random.fold_in(key, 17))
    middle = jax.random.permutation(first_key, OWNERS - 2) + 1
    chosen = jnp.concatenate([jnp.array([0, OWNERS - 1], dtype=jnp.int32), middle[:STEPS - 2].astype(jnp.int32)])
    return jax.random.permutation(second_key, chosen).astype(jnp.int32)


def place_ends(entries, stream_key, smallest, largest):
    shape = entries.shape
    place = [jax.random.randint(jax.random.fold_in(stream_key, axis), (), 0, shape[axis]) for axis in range(len(shape))]
    entries = entries.at[tuple(place)].set(smallest)
    longest = shape.index(max(shape))
    place[longest] = (place[longest] + 1) % shape[longest]
    return entries.at[tuple(place)].set(largest)


def block_levels(own_key, shape, shards, smallest, top_value):
    def one(position, shards_of):
        steps = jax.random.uniform(jax.random.fold_in(jax.random.fold_in(own_key, 6), position), (shards_of,), jnp.float32, smallest / len(shards), top_value / len(shards))
        return jnp.repeat(jnp.exp(steps), shape[position] // shards_of).reshape((-1,) + (1,) * (len(shape) - position - 1))

    gain = one(*shards[0])
    for cut in shards[1:]:
        gain = gain * one(*cut)
    return gain


def scatter_about(own_key, shape, deviation, bound, cuts=(), held_as=jnp.bfloat16):
    level = block_levels(own_key, shape, cuts, -0.22, 0.18) if cuts else 1.0
    drawn = jax.random.normal(own_key, shape, jnp.float32) * deviation * level
    return jnp.minimum(jnp.maximum(drawn, -bound), bound).astype(held_as)


def setup_inputs(seed: int = 0) -> dict:
    streams_of = jax.random.split(jax.random.key(seed), 8)
    return {
        "wavefield": scatter_about(streams_of[0], (SOURCES, 9, NX, NY, NZ), 1.0, 6.0, ((0, 8), (2, 4)), jnp.float32),
        "strain_bank": scatter_about(streams_of[1], (OWNERS, 6, NX, NY, NZ), 1.0, 6.0, ((0, 8), (2, 4))),
        "owners": draw_owners(jax.random.fold_in(streams_of[7], 71), 0),
        "region": place_ends(jax.random.randint(streams_of[3], (NX, NY, NZ), 0, REGIONS), jax.random.fold_in(streams_of[3], 1), 0, REGIONS - 1).astype(jnp.int32),
        "region_lambda": jnp.clip(jax.random.uniform(streams_of[4], (REGIONS,), jnp.float32, 1.0, 2.0), 1.0, 2.0),
        "region_mu": jnp.clip(jax.random.uniform(streams_of[5], (REGIONS,), jnp.float32, 0.5, 1.0), 0.5, 1.0),
        "region_buoyancy": jnp.clip(jax.random.uniform(streams_of[6], (REGIONS,), jnp.float32, 0.5, 1.0), 0.5, 1.0),
    }


step_size = 0.3
x_force_terms = (0, 5, 4)
y_force_terms = (5, 1, 3)
z_force_terms = (4, 3, 2)


def slab_of(values, along, start, length):
    slicer = [slice(None)] * values.ndim
    slicer[values.ndim + along] = slice(start, start + length)
    return values[tuple(slicer)]


def diff_valid(padded, along):
    length = padded.shape[along] - 4
    near = slab_of(padded, along, 3, length) - slab_of(padded, along, 1, length)
    far = slab_of(padded, along, 4, length) - slab_of(padded, along, 0, length)
    return (8.0 * near - far) / 12.0


def diff_zero(values, along):
    widths = [(0, 0)] * values.ndim
    widths[values.ndim + along] = (2, 2)
    return diff_valid(jnp.pad(values, widths), along)


def component(values, which):
    return values[..., which, :, :, :]


def pick_terms(values, order):
    return jnp.stack([component(values, which) for which in order], -4)


def stress_update(stress, grad_x, grad_y, grad_z, lame_first, shear):
    diagonal = [component(grad_x, 0), component(grad_y, 1), component(grad_z, 2)]
    divergence = diagonal[0] + diagonal[1] + diagonal[2]
    parts = [component(stress, which) + step_size * (lame_first * divergence + 2.0 * shear * diagonal[which]) for which in range(3)]
    parts.append(component(stress, 3) + step_size * shear * (component(grad_z, 1) + component(grad_y, 2)))
    parts.append(component(stress, 4) + step_size * shear * (component(grad_z, 0) + component(grad_x, 2)))
    parts.append(component(stress, 5) + step_size * shear * (component(grad_y, 0) + component(grad_x, 1)))
    return jnp.stack(parts, -4)


def correlate(stress, receiver, lame_first, shear):
    trace = component(stress, 0) + component(stress, 1) + component(stress, 2)
    theta = trace / (3.0 * lame_first + 2.0 * shear)
    recv_trace = receiver[0] + receiver[1] + receiver[2]
    term_lambda = step_size * theta * recv_trace
    inner = jnp.zeros_like(theta)
    for which in range(3):
        inner = inner + (component(stress, which) - lame_first * theta) / (2.0 * shear) * receiver[which]
    for which in range(3, 6):
        inner = inner + component(stress, which) / shear * receiver[which]
    term_mu = step_size * 2.0 * inner
    return term_lambda, term_mu


def reference(wavefield, strain_bank, owners, region, region_lambda, region_mu, region_buoyancy):
    lame_first = region_lambda[region]
    shear = region_mu[region]
    buoyancy = region_buoyancy[region]

    def one_source(carry, state):
        kernel_lambda, kernel_mu = carry
        for time_step in range(STEPS):
            velocity = state[0:3]
            stress = state[3:9]
            force = diff_zero(pick_terms(stress, x_force_terms), -3) + diff_zero(pick_terms(stress, y_force_terms), -2) + diff_zero(pick_terms(stress, z_force_terms), -1)
            velocity = velocity + step_size * buoyancy * force
            stress = stress_update(stress, diff_zero(velocity, -3), diff_zero(velocity, -2), diff_zero(velocity, -1), lame_first, shear)
            state = jnp.concatenate([velocity, stress], -4)
            receiver = lax.dynamic_index_in_dim(strain_bank, owners[time_step], 0, keepdims=False).astype(jnp.float32)
            term_lambda, term_mu = correlate(stress, receiver, lame_first, shear)
            kernel_lambda = kernel_lambda + term_lambda
            kernel_mu = kernel_mu + term_mu
        return (kernel_lambda, kernel_mu), state

    zeros = jnp.zeros(region.shape, jnp.float32)
    (kernel_lambda, kernel_mu), new_wavefield = lax.scan(one_source, (zeros, zeros), wavefield)
    return new_wavefield, kernel_lambda, kernel_mu
```

```python
import functools

import jax
import jax.numpy as jnp
from jax import lax
from jax.experimental import pallas as pl
from jax.experimental.pallas import tpu as pltpu
from jax.sharding import PartitionSpec as P

STEPS = 4
DT = 0.3
NEAR = 8.0 / 12.0
FAR = 1.0 / 12.0
MESH = pl.DeviceIdType.MESH

XX, XZ, XY, YY, ZZ, YZ = range(6)
BANK = (0, 4, 5, 1, 2, 3)
PAD = 8


def kernel(
    n, m, nx, ny, chunk, split,
    owners, t_lam, t_mu, t_buoy, region, wave, bank,
    out_wave, out_lam, out_mu,
    vel, sig, mat, swap, gather, terms, arrived,
    load_sem, store_sem, bank_sem,
    a2a_send, a2a_recv, g_send, g_recv, k_send, k_recv,
    vs_send, vs_recv, ss_send, ss_recv,
):
    me = lax.axis_index("src")
    pos = lax.axis_index("space")
    rows = ny // n
    first, last = pos == 0, pos == m - 1
    lower, upper = lax.rem(pos + m - 1, m), lax.rem(pos + 1, m)

    inside = (slice(2, 2 + nx), slice(PAD, PAD + ny))
    loads = []
    for src, dst in (
        (wave.at[3:4], sig.at[0, XX:XZ, inside[0], inside[1]]),
        (wave.at[7:9], sig.at[0, XZ:YY, inside[0], inside[1]]),
        (wave.at[4:7], sig.at[0, YY:, inside[0], inside[1]]),
        (wave.at[0:3], vel.at[0, :, inside[0], inside[1]]),
    ):
        loads.append(pltpu.make_async_copy(src, dst, load_sem.at[len(loads)]))
        loads[-1].start()
    own = pltpu.make_async_copy(bank.at[:, me], swap.at[me], bank_sem)
    own.start()

    barrier = pltpu.get_barrier_semaphore()
    for d in range(1, n):
        pl.semaphore_signal(barrier, inc=1, device_id={"src": lax.rem(me + d, n)}, device_id_type=MESH)
    for to in (lower, upper):
        pl.semaphore_signal(barrier, inc=1, device_id={"space": to}, device_id_type=MESH)
    pl.semaphore_wait(barrier, n - 1 + 2)

    swaps = []
    for d in range(1, n):
        peer = lax.rem(me + d, n)
        swaps.append(pltpu.make_async_remote_copy(
            src_ref=bank.at[:, peer], dst_ref=swap.at[me],
            send_sem=a2a_send.at[d], recv_sem=a2a_recv.at[d],
            device_id={"src": peer}, device_id_type=MESH))

    def halos(buf, t, send, recv):
        down = pltpu.make_async_remote_copy(
            src_ref=buf.at[t, 0:3, 2:4, inside[1]],
            dst_ref=buf.at[t, 0:3, nx + 2:nx + 4, inside[1]],
            send_sem=send.at[t, 0], recv_sem=recv.at[t, 0],
            device_id={"space": lower}, device_id_type=MESH)
        up = pltpu.make_async_remote_copy(
            src_ref=buf.at[t, 0:3, nx:nx + 2, inside[1]],
            dst_ref=buf.at[t, 0:3, 0:2, inside[1]],
            send_sem=send.at[t, 1], recv_sem=recv.at[t, 1],
            device_id={"space": upper}, device_id_type=MESH)
        return down, up

    def send_halos(pair):
        pl.when(jnp.logical_not(first))(lambda: pair[0].start())
        pl.when(jnp.logical_not(last))(lambda: pair[1].start())

    def take_halos(pair):
        pl.when(jnp.logical_not(last))(lambda: pair[0].wait_recv())
        pl.when(jnp.logical_not(first))(lambda: pair[1].wait_recv())

    def sent_halos(pair):
        pl.when(jnp.logical_not(first))(lambda: pair[0].wait_send())
        pl.when(jnp.logical_not(last))(lambda: pair[1].wait_send())

    s_halos = [halos(sig, t, ss_send, ss_recv) for t in range(STEPS)]
    v_halos = [halos(vel, t, vs_send, vs_recv) for t in range(1, STEPS + 1)]

    for copy in loads[:2]:
        copy.wait()
    send_halos(s_halos[0])
    for copy in swaps:
        copy.start()

    wide = vel.shape[-1]
    for buf, times in ((sig, range(STEPS)), (vel, range(1, STEPS + 1))):
        for t in times:
            count = buf.shape[1]
            edge = jnp.zeros((count, nx, PAD, wide), jnp.float32)
            buf[t, :, 2:nx + 2, 0:PAD, :] = edge
            buf[t, :, 2:nx + 2, PAD + ny:, :] = edge

            @pl.when(first)
            def _():
                buf[t, 0:3, 0:2, PAD:PAD + ny, :] = jnp.zeros((3, 2, ny, wide), jnp.float32)

            @pl.when(last)
            def _():
                buf[t, 0:3, nx + 2:, PAD:PAD + ny, :] = jnp.zeros((3, 2, ny, wide), jnp.float32)

    def materials(i, carry):
        label = region[i]
        found = [jnp.zeros(label.shape, jnp.float32) for _ in range(3)]
        for which in range(t_lam.shape[0]):
            hit = label == which
            found = [jnp.where(hit, table[which], old)
                     for table, old in zip((t_lam, t_mu, t_buoy), found)]
        for which in range(3):
            mat[which, i] = found[which]
        return carry

    lax.fori_loop(0, nx, materials, 0)
    for copy in loads[2:]:
        copy.wait()

    tall = ny // split
    lane = lax.broadcasted_iota(jnp.int32, (tall, wide), 1)

    def deriv_x(buf, t, c, i, y):
        at = lambda k: buf[t, c, i + 2 + k, PAD + y:PAD + y + tall, :]
        return at(1) - at(-1), at(2) - at(-2)

    def deriv_y(buf, t, c, i, y):
        at = lambda k: buf[t, c, i + 2, PAD + y + k:PAD + y + k + tall, :]
        return at(1) - at(-1), at(2) - at(-2)

    def deriv_z(buf, t, c, i, y):
        f = buf[t, c, i + 2, PAD + y:PAD + y + tall, :]

        def at(k):
            moved = pltpu.roll(f, (-k) % wide, 1)
            keep = lane < wide - k if k > 0 else lane >= -k
            return jnp.where(keep, moved, 0.0)

        return at(1) - at(-1), at(2) - at(-2)

    def total(*pairs):
        near, far = pairs[0]
        for a, b in pairs[1:]:
            near, far = near + a, far + b
        return NEAR * near - FAR * far

    def velocity_row(t, i):
        for y in range(0, ny, tall):
            here = slice(PAD + y, PAD + y + tall)
            gain = DT * mat[2, i, y:y + tall, :]
            for c, (a, b, d) in enumerate(((XX, XY, XZ), (XY, YY, YZ), (XZ, YZ, ZZ))):
                force = total(deriv_x(sig, t, a, i, y), deriv_y(sig, t, b, i, y), deriv_z(sig, t, d, i, y))
                vel[t + 1, c, i + 2, here, :] = vel[t, c, i + 2, here, :] + gain * force

    def stress_row(t, i):
        s = t + 1
        for y in range(0, ny, tall):
            here = slice(PAD + y, PAD + y + tall)
            lam = DT * mat[0, i, y:y + tall, :]
            mu = DT * mat[1, i, y:y + tall, :]

            def put(c, change):
                sig[s, c, i + 2, here, :] = sig[t, c, i + 2, here, :] + change

            gx = total(deriv_x(vel, s, 0, i, y))
            gy = total(deriv_y(vel, s, 1, i, y))
            gz = total(deriv_z(vel, s, 2, i, y))
            div = lam * (gx + gy + gz)
            put(XX, div + 2.0 * mu * gx)
            put(YY, div + 2.0 * mu * gy)
            put(ZZ, div + 2.0 * mu * gz)
            put(YZ, mu * total(deriv_z(vel, s, 1, i, y), deriv_y(vel, s, 2, i, y)))
            put(XZ, mu * total(deriv_z(vel, s, 0, i, y), deriv_x(vel, s, 2, i, y)))
            put(XY, mu * total(deriv_y(vel, s, 0, i, y), deriv_x(vel, s, 1, i, y)))

    def over(row, t, start, stop):
        def body(i, carry):
            row(t, i)
            return carry
        lax.fori_loop(start, stop, body, 0)

    spreads = []
    for d in range(1, n):
        peer = lax.rem(me + d, n)
        spreads.append(pltpu.make_async_remote_copy(
            src_ref=gather.at[me], dst_ref=gather.at[me],
            send_sem=g_send.at[d], recv_sem=g_recv.at[d],
            device_id={"src": peer}, device_id_type=MESH))

    for t in range(STEPS):
        over(velocity_row, t, 2, nx - 2)
        take_halos(s_halos[t])
        over(velocity_row, t, 0, 2)
        over(velocity_row, t, nx - 2, nx)
        send_halos(v_halos[t])
        over(stress_row, t, 2, nx - 2)
        if t == 0:
            own.wait()
            for copy in swaps:
                copy.wait()
            for s in range(STEPS):
                gather[me, s] = swap[owners[s]]
            for copy in spreads:
                copy.start()
        take_halos(v_halos[t])
        over(stress_row, t, 0, 2)
        over(stress_row, t, nx - 2, nx)
        if t + 1 < STEPS:
            send_halos(s_halos[t + 1])

    stores = []
    for src, dst in (
        (sig.at[STEPS, XX:XZ, inside[0], inside[1]], out_wave.at[3:4]),
        (sig.at[STEPS, XZ:YY, inside[0], inside[1]], out_wave.at[7:9]),
        (sig.at[STEPS, YY:, inside[0], inside[1]], out_wave.at[4:7]),
        (vel.at[STEPS, :, inside[0], inside[1]], out_wave.at[0:3]),
    ):
        stores.append(pltpu.make_async_copy(src, dst, store_sem.at[len(stores)]))
        stores[-1].start()

    for copy in spreads:
        copy.wait()

    per_row = ny // chunk

    def correlate(i, carry):
        for part in range(per_row):
            y = part * chunk
            j = i * per_row + part
            lam = mat[0, i, y:y + chunk, :]
            mu = mat[1, i, y:y + chunk, :]
            stiff = 1.0 / (3.0 * lam + 2.0 * mu)
            soft = DT / mu
            k_lam = jnp.zeros(lam.shape, jnp.float32)
            k_mu = jnp.zeros(lam.shape, jnp.float32)
            for t in range(STEPS):
                s = [sig[t + 1, c, i + 2, PAD + y:PAD + y + chunk, :] for c in range(6)]
                r = [gather[j, t, BANK[c]].astype(jnp.float32) for c in range(6)]
                theta = (s[XX] + s[YY] + s[ZZ]) * stiff
                trace = theta * (r[XX] + r[YY] + r[ZZ])
                k_lam = k_lam + trace
                k_mu = (k_mu + s[XX] * r[XX] + s[YY] * r[YY] + s[ZZ] * r[ZZ] - lam * trace
                        + 2.0 * (s[YZ] * r[YZ] + s[XZ] * r[XZ] + s[XY] * r[XY]))
            k_lam = DT * k_lam
            k_mu = soft * k_mu
            for z in range(chunk // rows):
                terms[y // rows + z, 0, i] = k_lam[z * rows:(z + 1) * rows]
                terms[y // rows + z, 1, i] = k_mu[z * rows:(z + 1) * rows]
        return carry

    lax.fori_loop(0, nx, correlate, 0)

    sums = []
    for d in range(1, n):
        peer = lax.rem(me + d, n)
        sums.append(pltpu.make_async_remote_copy(
            src_ref=terms.at[peer], dst_ref=arrived.at[me],
            send_sem=k_send.at[d], recv_sem=k_recv.at[d],
            device_id={"src": peer}, device_id_type=MESH))
        sums[-1].start()
    for pair in s_halos + v_halos:
        sent_halos(pair)
    arrived[me] = terms[me]
    for copy in sums:
        copy.wait()
    for which, out in ((0, out_lam), (1, out_mu)):
        acc = arrived[0, which]
        for d in range(1, n):
            acc = acc + arrived[d, which]
        out[...] = acc
    for copy in stores:
        copy.wait()


def solution(mesh):
    n, m = mesh.shape["src"], mesh.shape["space"]

    def local(wavefield, strain_bank, owners, region, region_lambda, region_mu, region_buoyancy):
        nx, ny, nz = region.shape
        chunk = nx * ny // n
        rows = ny // n
        bank = strain_bank[0].reshape(6, n, chunk, nz)
        hbm = pl.BlockSpec(memory_space=pl.ANY)
        vmem = pl.BlockSpec(memory_space=pltpu.VMEM)
        smem = pl.BlockSpec(memory_space=pltpu.SMEM)
        dma = pltpu.SemaphoreType.DMA
        new, k_lam, k_mu = pl.pallas_call(
            functools.partial(kernel, n, m, nx, ny, chunk, 2),
            out_shape=(
                jax.ShapeDtypeStruct((9, nx, ny, nz), jnp.float32),
                jax.ShapeDtypeStruct((nx, rows, nz), jnp.float32),
                jax.ShapeDtypeStruct((nx, rows, nz), jnp.float32),
            ),
            in_specs=[smem, smem, smem, smem, vmem, hbm, hbm],
            out_specs=(hbm, vmem, vmem),
            scratch_shapes=[
                pltpu.VMEM((STEPS + 1, 3, nx + 4, ny + 2 * PAD, nz), jnp.float32),
                pltpu.VMEM((STEPS + 1, 6, nx + 4, ny + 2 * PAD, nz), jnp.float32),
                pltpu.VMEM((3, nx, ny, nz), jnp.float32),
                pltpu.VMEM((n, 6, chunk, nz), jnp.bfloat16),
                pltpu.VMEM((n, STEPS, 6, chunk, nz), jnp.bfloat16),
                pltpu.VMEM((n, 2, nx, rows, nz), jnp.float32),
                pltpu.VMEM((n, 2, nx, rows, nz), jnp.float32),
                dma((4,)), dma((4,)), dma,
                dma((n,)), dma((n,)), dma((n,)), dma((n,)), dma((n,)), dma((n,)),
                dma((STEPS + 1, 2)), dma((STEPS + 1, 2)), dma((STEPS + 1, 2)), dma((STEPS + 1, 2)),
            ],
            compiler_params=pltpu.CompilerParams(
                collective_id=0, has_side_effects=True, vmem_limit_bytes=56 * 1024 * 1024
            ),
        )(owners, region_lambda, region_mu, region_buoyancy, region, wavefield[0], bank)
        return new[None], k_lam, k_mu

    in_specs = (
        P("src", None, "space", None, None),
        P("src", None, "space", None, None),
        P(),
        P("space", None, None),
        P(),
        P(),
        P(),
    )
    out_specs = (
        P("src", None, "space", None, None),
        P("space", "src", None),
        P("space", "src", None),
    )
    return jax.shard_map(local, mesh=mesh, in_specs=in_specs, out_specs=out_specs, check_vma=False)
```

```python
import functools

import jax
import jax.numpy as jnp
from jax import lax
from jax.experimental import pallas as pl
from jax.experimental.pallas import tpu as pltpu
from jax.sharding import PartitionSpec as P

STEPS = 4
DT = 0.3
NEAR = 8.0 / 12.0
FAR = 1.0 / 12.0
MESH = pl.DeviceIdType.MESH

XX, XZ, XY, YY, ZZ, YZ = range(6)
BANK = (0, 4, 5, 1, 2, 3)
PAD = 8


def kernel(
    n, m, nx, ny, chunk, split,
    owners, t_lam, t_mu, t_buoy, region, wave, bank,
    out_wave, out_lam, out_mu,
    vel, sig, mat, swap, gather, terms, arrived,
    load_sem, store_sem, bank_sem,
    a2a_send, a2a_recv, c_send, c_recv, p_send, p_recv, b_send, b_recv, k_send, k_recv,
    vs_send, vs_recv, ss_send, ss_recv,
):
    me = lax.axis_index("src")
    pos = lax.axis_index("space")
    rows = ny // n
    first, last = pos == 0, pos == m - 1
    lower, upper = lax.rem(pos + m - 1, m), lax.rem(pos + 1, m)

    inside = (slice(2, 2 + nx), slice(PAD, PAD + ny))
    loads = []
    for src, dst in (
        (wave.at[3:4], sig.at[0, XX:XZ, inside[0], inside[1]]),
        (wave.at[7:9], sig.at[0, XZ:YY, inside[0], inside[1]]),
        (wave.at[4:7], sig.at[0, YY:, inside[0], inside[1]]),
        (wave.at[0:3], vel.at[0, :, inside[0], inside[1]]),
    ):
        loads.append(pltpu.make_async_copy(src, dst, load_sem.at[len(loads)]))
        loads[-1].start()
    own = pltpu.make_async_copy(bank.at[:, me], swap.at[me], bank_sem)
    own.start()

    barrier = pltpu.get_barrier_semaphore()
    for d in range(1, n):
        pl.semaphore_signal(barrier, inc=1, device_id={"src": lax.rem(me + d, n)}, device_id_type=MESH)
    for to in (lower, upper):
        pl.semaphore_signal(barrier, inc=1, device_id={"space": to}, device_id_type=MESH)
    pl.semaphore_wait(barrier, n - 1 + 2)

    swaps = []
    for d in range(1, n):
        peer = lax.rem(me + d, n)
        swaps.append(pltpu.make_async_remote_copy(
            src_ref=bank.at[:, peer], dst_ref=swap.at[me],
            send_sem=a2a_send.at[d], recv_sem=a2a_recv.at[d],
            device_id={"src": peer}, device_id_type=MESH))

    def halos(buf, t, send, recv):
        down = pltpu.make_async_remote_copy(
            src_ref=buf.at[t, 0:3, 2:4, inside[1]],
            dst_ref=buf.at[t, 0:3, nx + 2:nx + 4, inside[1]],
            send_sem=send.at[t, 0], recv_sem=recv.at[t, 0],
            device_id={"space": lower}, device_id_type=MESH)
        up = pltpu.make_async_remote_copy(
            src_ref=buf.at[t, 0:3, nx:nx + 2, inside[1]],
            dst_ref=buf.at[t, 0:3, 0:2, inside[1]],
            send_sem=send.at[t, 1], recv_sem=recv.at[t, 1],
            device_id={"space": upper}, device_id_type=MESH)
        return down, up

    def send_halos(pair):
        pl.when(jnp.logical_not(first))(lambda: pair[0].start())
        pl.when(jnp.logical_not(last))(lambda: pair[1].start())

    def take_halos(pair):
        pl.when(jnp.logical_not(last))(lambda: pair[0].wait_recv())
        pl.when(jnp.logical_not(first))(lambda: pair[1].wait_recv())

    def sent_halos(pair):
        pl.when(jnp.logical_not(first))(lambda: pair[0].wait_send())
        pl.when(jnp.logical_not(last))(lambda: pair[1].wait_send())

    s_halos = [halos(sig, t, ss_send, ss_recv) for t in range(STEPS)]
    v_halos = [halos(vel, t, vs_send, vs_recv) for t in range(1, STEPS + 1)]

    for copy in loads[:2]:
        copy.wait()
    send_halos(s_halos[0])
    for copy in swaps:
        copy.start()

    wide = vel.shape[-1]
    for buf, times in ((sig, range(STEPS)), (vel, range(1, STEPS + 1))):
        for t in times:
            count = buf.shape[1]
            edge = jnp.zeros((count, nx, PAD, wide), jnp.float32)
            buf[t, :, 2:nx + 2, 0:PAD, :] = edge
            buf[t, :, 2:nx + 2, PAD + ny:, :] = edge

            @pl.when(first)
            def _():
                buf[t, 0:3, 0:2, PAD:PAD + ny, :] = jnp.zeros((3, 2, ny, wide), jnp.float32)

            @pl.when(last)
            def _():
                buf[t, 0:3, nx + 2:, PAD:PAD + ny, :] = jnp.zeros((3, 2, ny, wide), jnp.float32)

    def materials(i, carry):
        label = region[i]
        found = [jnp.zeros(label.shape, jnp.float32) for _ in range(3)]
        for which in range(t_lam.shape[0]):
            hit = label == which
            found = [jnp.where(hit, table[which], old)
                     for table, old in zip((t_lam, t_mu, t_buoy), found)]
        for which in range(3):
            mat[which, i] = found[which]
        return carry

    lax.fori_loop(0, nx, materials, 0)
    for copy in loads[2:]:
        copy.wait()

    tall = ny // split
    lane = lax.broadcasted_iota(jnp.int32, (tall, wide), 1)

    def deriv_x(buf, t, c, i, y):
        at = lambda k: buf[t, c, i + 2 + k, PAD + y:PAD + y + tall, :]
        return at(1) - at(-1), at(2) - at(-2)

    def deriv_y(buf, t, c, i, y):
        at = lambda k: buf[t, c, i + 2, PAD + y + k:PAD + y + k + tall, :]
        return at(1) - at(-1), at(2) - at(-2)

    def deriv_z(buf, t, c, i, y):
        f = buf[t, c, i + 2, PAD + y:PAD + y + tall, :]

        def at(k):
            moved = pltpu.roll(f, (-k) % wide, 1)
            keep = lane < wide - k if k > 0 else lane >= -k
            return jnp.where(keep, moved, 0.0)

        return at(1) - at(-1), at(2) - at(-2)

    def total(*pairs):
        near, far = pairs[0]
        for a, b in pairs[1:]:
            near, far = near + a, far + b
        return NEAR * near - FAR * far

    def velocity_row(t, i):
        for y in range(0, ny, tall):
            here = slice(PAD + y, PAD + y + tall)
            gain = DT * mat[2, i, y:y + tall, :]
            for c, (a, b, d) in enumerate(((XX, XY, XZ), (XY, YY, YZ), (XZ, YZ, ZZ))):
                force = total(deriv_x(sig, t, a, i, y), deriv_y(sig, t, b, i, y), deriv_z(sig, t, d, i, y))
                vel[t + 1, c, i + 2, here, :] = vel[t, c, i + 2, here, :] + gain * force

    def stress_row(t, i):
        s = t + 1
        for y in range(0, ny, tall):
            here = slice(PAD + y, PAD + y + tall)
            lam = DT * mat[0, i, y:y + tall, :]
            mu = DT * mat[1, i, y:y + tall, :]

            def put(c, change):
                sig[s, c, i + 2, here, :] = sig[t, c, i + 2, here, :] + change

            gx = total(deriv_x(vel, s, 0, i, y))
            gy = total(deriv_y(vel, s, 1, i, y))
            gz = total(deriv_z(vel, s, 2, i, y))
            div = lam * (gx + gy + gz)
            put(XX, div + 2.0 * mu * gx)
            put(YY, div + 2.0 * mu * gy)
            put(ZZ, div + 2.0 * mu * gz)
            put(YZ, mu * total(deriv_z(vel, s, 1, i, y), deriv_y(vel, s, 2, i, y)))
            put(XZ, mu * total(deriv_z(vel, s, 0, i, y), deriv_x(vel, s, 2, i, y)))
            put(XY, mu * total(deriv_y(vel, s, 0, i, y), deriv_x(vel, s, 1, i, y)))

    def over(row, t, start, stop):
        def body(i, carry):
            row(t, i)
            return carry
        lax.fori_loop(start, stop, body, 0)

    line, side = me // 2, lax.rem(me, 2)
    lines = n // 2
    partner = me + 1 - 2 * side
    ways = (1, -1)
    most, rest = pl.ds(0, STEPS - 1), pl.ds(STEPS - 1, 1)
    items = ((most, False), (rest, False), (rest, True))

    def place(origin, swapped):
        return origin * 2 + (1 - side if swapped else side)

    def link(k, w, hop, origin):
        slots, swapped = items[k]
        part = gather.at[place(origin, swapped), slots]
        return pltpu.make_async_remote_copy(
            src_ref=part, dst_ref=part,
            send_sem=c_send.at[k, w, hop], recv_sem=c_recv.at[k, w, hop],
            device_id={"src": me + 2 * ways[w]}, device_id_type=MESH)

    def across(w, hop, origin):
        part = gather.at[place(origin, False), most]
        other = gather.at[place(origin, True), most]
        send = pltpu.make_async_remote_copy(
            src_ref=part, dst_ref=part, send_sem=p_send.at[w, hop], recv_sem=p_recv.at[w, hop],
            device_id={"src": partner}, device_id_type=MESH)
        take = pltpu.make_async_remote_copy(
            src_ref=other, dst_ref=other, send_sem=p_send.at[w, hop], recv_sem=p_recv.at[w, hop],
            device_id={"src": partner}, device_id_type=MESH)
        return send, take

    def across_rest(whose):
        part = gather.at[whose, rest]
        return pltpu.make_async_remote_copy(
            src_ref=part, dst_ref=part, send_sem=b_send, recv_sem=b_recv,
            device_id={"src": partner}, device_id_type=MESH)

    def exists(at):
        return jnp.logical_and(at >= 0, at < lines)

    def each_link(k, hop, act):
        for w, way in enumerate(ways):
            origin = line - way * hop
            pl.when(jnp.logical_and(exists(origin), exists(line + way)))(
                lambda w=w, origin=origin: act(link(k, w, hop, origin)))

    def take_link(k, hop):
        for w, way in enumerate(ways):
            origin = line - way * (hop + 1)
            pl.when(exists(origin))(lambda w=w, origin=origin: link(k, w, hop, origin).wait_recv())

    def each_across(hop, act):
        for w, way in enumerate(ways):
            origin = line - way * (hop + 1)
            pl.when(exists(origin))(lambda w=w, origin=origin: act(*across(w, hop + 1, origin)))

    start = lambda copy: copy.start()

    def begin():
        own.wait()
        for copy in swaps:
            copy.wait()
        for s in range(STEPS):
            gather[me, s] = swap[owners[s]]
        across_rest(me).start()
        each_link(0, 0, start)
        across(0, 0, line)[0].start()
        each_link(1, 0, start)

    def along_most(hop):
        if hop == 0:
            across_rest(partner).wait_recv()
            each_link(2, 0, start)
        take_link(0, hop)
        if hop + 1 < lines - 1:
            each_link(0, hop + 1, start)
        each_across(hop, lambda send, take: send.start())

    def along_rest(hop):
        for k in (1, 2):
            take_link(k, hop)
            if hop + 1 < lines - 1:
                each_link(k, hop + 1, start)

    def settle(send, take):
        send.wait_send()
        take.wait_recv()

    def finish():
        across_rest(me).wait_send()
        send, take = across(0, 0, line)
        send.wait_send()
        take.wait_recv()
        for hop in range(lines - 1):
            for k in range(3):
                each_link(k, hop, lambda copy: copy.wait_send())
            each_across(hop, settle)

    pumps = [begin]
    for hop in range(lines - 1):
        pumps.append(functools.partial(along_most, hop))
        pumps.append(functools.partial(along_rest, hop))

    for t in range(STEPS):
        over(velocity_row, t, 2, nx - 2)
        take_halos(s_halos[t])
        over(velocity_row, t, 0, 2)
        over(velocity_row, t, nx - 2, nx)
        send_halos(v_halos[t])
        if t > 0:
            pumps.pop(0)()
        over(stress_row, t, 2, nx - 2)
        take_halos(v_halos[t])
        over(stress_row, t, 0, 2)
        over(stress_row, t, nx - 2, nx)
        if t + 1 < STEPS:
            send_halos(s_halos[t + 1])
            pumps.pop(0)()

    stores = []
    for src, dst in (
        (sig.at[STEPS, XX:XZ, inside[0], inside[1]], out_wave.at[3:4]),
        (sig.at[STEPS, XZ:YY, inside[0], inside[1]], out_wave.at[7:9]),
        (sig.at[STEPS, YY:, inside[0], inside[1]], out_wave.at[4:7]),
        (vel.at[STEPS, :, inside[0], inside[1]], out_wave.at[0:3]),
    ):
        stores.append(pltpu.make_async_copy(src, dst, store_sem.at[len(stores)]))
        stores[-1].start()

    for pump in pumps:
        pump()
    finish()

    per_row = ny // chunk

    def correlate(i, carry):
        for part in range(per_row):
            y = part * chunk
            j = i * per_row + part
            lam = mat[0, i, y:y + chunk, :]
            mu = mat[1, i, y:y + chunk, :]
            stiff = 1.0 / (3.0 * lam + 2.0 * mu)
            soft = DT / mu
            k_lam = jnp.zeros(lam.shape, jnp.float32)
            k_mu = jnp.zeros(lam.shape, jnp.float32)
            for t in range(STEPS):
                s = [sig[t + 1, c, i + 2, PAD + y:PAD + y + chunk, :] for c in range(6)]
                r = [gather[j, t, BANK[c]].astype(jnp.float32) for c in range(6)]
                theta = (s[XX] + s[YY] + s[ZZ]) * stiff
                trace = theta * (r[XX] + r[YY] + r[ZZ])
                k_lam = k_lam + trace
                k_mu = (k_mu + s[XX] * r[XX] + s[YY] * r[YY] + s[ZZ] * r[ZZ] - lam * trace
                        + 2.0 * (s[YZ] * r[YZ] + s[XZ] * r[XZ] + s[XY] * r[XY]))
            k_lam = DT * k_lam
            k_mu = soft * k_mu
            for z in range(chunk // rows):
                terms[y // rows + z, 0, i] = k_lam[z * rows:(z + 1) * rows]
                terms[y // rows + z, 1, i] = k_mu[z * rows:(z + 1) * rows]
        return carry

    lax.fori_loop(0, nx, correlate, 0)

    sums = []
    for d in range(1, n):
        peer = lax.rem(me + d, n)
        sums.append(pltpu.make_async_remote_copy(
            src_ref=terms.at[peer], dst_ref=arrived.at[me],
            send_sem=k_send.at[d], recv_sem=k_recv.at[d],
            device_id={"src": peer}, device_id_type=MESH))
        sums[-1].start()
    for pair in s_halos + v_halos:
        sent_halos(pair)
    arrived[me] = terms[me]
    for copy in sums:
        copy.wait()
    for which, out in ((0, out_lam), (1, out_mu)):
        acc = arrived[0, which]
        for d in range(1, n):
            acc = acc + arrived[d, which]
        out[...] = acc
    for copy in stores:
        copy.wait()


def solution(mesh):
    n, m = mesh.shape["src"], mesh.shape["space"]

    def local(wavefield, strain_bank, owners, region, region_lambda, region_mu, region_buoyancy):
        nx, ny, nz = region.shape
        chunk = nx * ny // n
        rows = ny // n
        bank = strain_bank[0].reshape(6, n, chunk, nz)
        hbm = pl.BlockSpec(memory_space=pl.ANY)
        vmem = pl.BlockSpec(memory_space=pltpu.VMEM)
        smem = pl.BlockSpec(memory_space=pltpu.SMEM)
        dma = pltpu.SemaphoreType.DMA
        new, k_lam, k_mu = pl.pallas_call(
            functools.partial(kernel, n, m, nx, ny, chunk, 2),
            out_shape=(
                jax.ShapeDtypeStruct((9, nx, ny, nz), jnp.float32),
                jax.ShapeDtypeStruct((nx, rows, nz), jnp.float32),
                jax.ShapeDtypeStruct((nx, rows, nz), jnp.float32),
            ),
            in_specs=[smem, smem, smem, smem, vmem, hbm, hbm],
            out_specs=(hbm, vmem, vmem),
            scratch_shapes=[
                pltpu.VMEM((STEPS + 1, 3, nx + 4, ny + 2 * PAD, nz), jnp.float32),
                pltpu.VMEM((STEPS + 1, 6, nx + 4, ny + 2 * PAD, nz), jnp.float32),
                pltpu.VMEM((3, nx, ny, nz), jnp.float32),
                pltpu.VMEM((n, 6, chunk, nz), jnp.bfloat16),
                pltpu.VMEM((n, STEPS, 6, chunk, nz), jnp.bfloat16),
                pltpu.VMEM((n, 2, nx, rows, nz), jnp.float32),
                pltpu.VMEM((n, 2, nx, rows, nz), jnp.float32),
                dma((4,)), dma((4,)), dma,
                dma((n,)), dma((n,)), dma((3, 2, n // 2)), dma((3, 2, n // 2)),
                dma((2, n // 2)), dma((2, n // 2)), dma, dma, dma((n,)), dma((n,)),
                dma((STEPS + 1, 2)), dma((STEPS + 1, 2)), dma((STEPS + 1, 2)), dma((STEPS + 1, 2)),
            ],
            compiler_params=pltpu.CompilerParams(
                collective_id=0, has_side_effects=True, vmem_limit_bytes=56 * 1024 * 1024
            ),
        )(owners, region_lambda, region_mu, region_buoyancy, region, wavefield[0], bank)
        return new[None], k_lam, k_mu

    in_specs = (
        P("src", None, "space", None, None),
        P("src", None, "space", None, None),
        P(),
        P("space", None, None),
        P(),
        P(),
        P(),
    )
    out_specs = (
        P("src", None, "space", None, None),
        P("space", "src", None),
        P("space", "src", None),
    )
    return jax.shard_map(local, mesh=mesh, in_specs=in_specs, out_specs=out_specs, check_vma=False)
```

```python
import functools

import jax
import jax.numpy as jnp
from jax import lax
from jax.experimental import pallas as pl
from jax.experimental.pallas import tpu as pltpu
from jax.sharding import PartitionSpec as P

STEPS = 4
DT = 0.3
NEAR = 8.0 / 12.0
FAR = 1.0 / 12.0
MESH = pl.DeviceIdType.MESH

XX, XZ, XY, YY, ZZ, YZ = range(6)
BANK = (0, 4, 5, 1, 2, 3)
PAD = 8


def kernel(
    n, m, nx, ny, chunk, split,
    owners, t_lam, t_mu, t_buoy, region, wave, bank,
    out_wave, out_lam, out_mu,
    vel, sig, mat, swap, gather, terms, arrived,
    load_sem, store_sem, bank_sem,
    a2a_send, a2a_recv, c_send, c_recv, p_send, p_recv, b_send, b_recv, k_send, k_recv,
    vs_send, vs_recv, ss_send, ss_recv,
):
    me = lax.axis_index("src")
    pos = lax.axis_index("space")
    rows = ny // n
    first, last = pos == 0, pos == m - 1
    lower, upper = lax.rem(pos + m - 1, m), lax.rem(pos + 1, m)

    inside = (slice(2, 2 + nx), slice(PAD, PAD + ny))
    loads = []
    for src, dst in (
        (wave.at[3:4], sig.at[0, XX:XZ, inside[0], inside[1]]),
        (wave.at[7:9], sig.at[0, XZ:YY, inside[0], inside[1]]),
        (wave.at[4:7], sig.at[0, YY:, inside[0], inside[1]]),
        (wave.at[0:3], vel.at[0, :, inside[0], inside[1]]),
    ):
        loads.append(pltpu.make_async_copy(src, dst, load_sem.at[len(loads)]))
        loads[-1].start()
    own = pltpu.make_async_copy(bank.at[:, me], swap.at[me], bank_sem)
    own.start()

    barrier = pltpu.get_barrier_semaphore()
    for d in range(1, n):
        pl.semaphore_signal(barrier, inc=1, device_id={"src": lax.rem(me + d, n)}, device_id_type=MESH)
    for to in (lower, upper):
        pl.semaphore_signal(barrier, inc=1, device_id={"space": to}, device_id_type=MESH)
    pl.semaphore_wait(barrier, n - 1 + 2)

    swaps = []
    for d in range(1, n):
        peer = lax.rem(me + d, n)
        swaps.append(pltpu.make_async_remote_copy(
            src_ref=bank.at[:, peer], dst_ref=swap.at[me],
            send_sem=a2a_send.at[d], recv_sem=a2a_recv.at[d],
            device_id={"src": peer}, device_id_type=MESH))

    odd = lax.rem(pos, 2)
    has_far = jnp.where(odd == 1, pos, m - 1 - pos) < m - 1
    near_rows, far_rows = (1 - odd) * (nx - 2), odd * (nx - 2)

    def halos(buf, t, send, recv):
        near = pltpu.make_async_remote_copy(
            src_ref=buf.at[t, 0:3, pl.ds(near_rows + 2, 2), inside[1]],
            dst_ref=buf.at[t, 0:3, pl.ds(odd * (nx + 2), 2), inside[1]],
            send_sem=send.at[t, 0], recv_sem=recv.at[t, 0],
            device_id={"space": pos + 1 - 2 * odd}, device_id_type=MESH)
        far = pltpu.make_async_remote_copy(
            src_ref=buf.at[t, 0:3, pl.ds(far_rows + 2, 2), inside[1]],
            dst_ref=buf.at[t, 0:3, pl.ds((1 - odd) * (nx + 2), 2), inside[1]],
            send_sem=send.at[t, 1], recv_sem=recv.at[t, 1],
            device_id={"space": lax.rem(pos + m - 1 + 2 * odd, m)}, device_id_type=MESH)
        return near, far

    def sent_halos(pair):
        pair[0].wait_send()
        pl.when(has_far)(lambda: pair[1].wait_send())

    s_halos = [halos(sig, t, ss_send, ss_recv) for t in range(STEPS)]
    v_halos = [halos(vel, t, vs_send, vs_recv) for t in range(1, STEPS + 1)]

    for copy in loads[:2]:
        copy.wait()
    s_halos[0][0].start()
    pl.when(has_far)(lambda: s_halos[0][1].start())
    for copy in swaps:
        copy.start()

    wide = vel.shape[-1]
    for buf, times in ((sig, range(STEPS)), (vel, range(1, STEPS + 1))):
        for t in times:
            count = buf.shape[1]
            edge = jnp.zeros((count, nx, PAD, wide), jnp.float32)
            buf[t, :, 2:nx + 2, 0:PAD, :] = edge
            buf[t, :, 2:nx + 2, PAD + ny:, :] = edge

            @pl.when(first)
            def _():
                buf[t, 0:3, 0:2, PAD:PAD + ny, :] = jnp.zeros((3, 2, ny, wide), jnp.float32)

            @pl.when(last)
            def _():
                buf[t, 0:3, nx + 2:, PAD:PAD + ny, :] = jnp.zeros((3, 2, ny, wide), jnp.float32)

    def materials(i, carry):
        label = region[i]
        found = [jnp.zeros(label.shape, jnp.float32) for _ in range(3)]
        for which in range(t_lam.shape[0]):
            hit = label == which
            found = [jnp.where(hit, table[which], old)
                     for table, old in zip((t_lam, t_mu, t_buoy), found)]
        for which in range(3):
            mat[which, i] = found[which]
        return carry

    lax.fori_loop(0, nx, materials, 0)
    for copy in loads[2:]:
        copy.wait()

    tall = ny // split
    lane = lax.broadcasted_iota(jnp.int32, (tall, wide), 1)

    def deriv_x(buf, t, c, i, y):
        at = lambda k: buf[t, c, i + 2 + k, PAD + y:PAD + y + tall, :]
        return at(1) - at(-1), at(2) - at(-2)

    def deriv_y(buf, t, c, i, y):
        at = lambda k: buf[t, c, i + 2, PAD + y + k:PAD + y + k + tall, :]
        return at(1) - at(-1), at(2) - at(-2)

    def deriv_z(buf, t, c, i, y):
        f = buf[t, c, i + 2, PAD + y:PAD + y + tall, :]

        def at(k):
            moved = pltpu.roll(f, (-k) % wide, 1)
            keep = lane < wide - k if k > 0 else lane >= -k
            return jnp.where(keep, moved, 0.0)

        return at(1) - at(-1), at(2) - at(-2)

    def total(*pairs):
        near, far = pairs[0]
        for a, b in pairs[1:]:
            near, far = near + a, far + b
        return NEAR * near - FAR * far

    def velocity_row(t, i):
        for y in range(0, ny, tall):
            here = slice(PAD + y, PAD + y + tall)
            gain = DT * mat[2, i, y:y + tall, :]
            for c, (a, b, d) in enumerate(((XX, XY, XZ), (XY, YY, YZ), (XZ, YZ, ZZ))):
                force = total(deriv_x(sig, t, a, i, y), deriv_y(sig, t, b, i, y), deriv_z(sig, t, d, i, y))
                vel[t + 1, c, i + 2, here, :] = vel[t, c, i + 2, here, :] + gain * force

    def stress_row(t, i):
        s = t + 1
        for y in range(0, ny, tall):
            here = slice(PAD + y, PAD + y + tall)
            lam = DT * mat[0, i, y:y + tall, :]
            mu = DT * mat[1, i, y:y + tall, :]

            def put(c, change):
                sig[s, c, i + 2, here, :] = sig[t, c, i + 2, here, :] + change

            gx = total(deriv_x(vel, s, 0, i, y))
            gy = total(deriv_y(vel, s, 1, i, y))
            gz = total(deriv_z(vel, s, 2, i, y))
            div = lam * (gx + gy + gz)
            put(XX, div + 2.0 * mu * gx)
            put(YY, div + 2.0 * mu * gy)
            put(ZZ, div + 2.0 * mu * gz)
            put(YZ, mu * total(deriv_z(vel, s, 1, i, y), deriv_y(vel, s, 2, i, y)))
            put(XZ, mu * total(deriv_z(vel, s, 0, i, y), deriv_x(vel, s, 2, i, y)))
            put(XY, mu * total(deriv_y(vel, s, 0, i, y), deriv_x(vel, s, 1, i, y)))

    def over(row, t, start, stop):
        def body(i, carry):
            row(t, start + i)
            return carry
        lax.fori_loop(0, nx - 4 if isinstance(start, int) else 2, body, 0)

    line, side = me // 2, lax.rem(me, 2)
    lines = n // 2
    partner = me + 1 - 2 * side
    ways = (1, -1)
    most, rest = pl.ds(0, STEPS - 1), pl.ds(STEPS - 1, 1)
    items = ((most, False), (rest, False), (rest, True))

    def place(origin, swapped):
        return origin * 2 + (1 - side if swapped else side)

    def link(k, w, hop, origin):
        slots, swapped = items[k]
        part = gather.at[place(origin, swapped), slots]
        return pltpu.make_async_remote_copy(
            src_ref=part, dst_ref=part,
            send_sem=c_send.at[k, w, hop], recv_sem=c_recv.at[k, w, hop],
            device_id={"src": me + 2 * ways[w]}, device_id_type=MESH)

    def across(w, hop, origin):
        part = gather.at[place(origin, False), most]
        other = gather.at[place(origin, True), most]
        send = pltpu.make_async_remote_copy(
            src_ref=part, dst_ref=part, send_sem=p_send.at[w, hop], recv_sem=p_recv.at[w, hop],
            device_id={"src": partner}, device_id_type=MESH)
        take = pltpu.make_async_remote_copy(
            src_ref=other, dst_ref=other, send_sem=p_send.at[w, hop], recv_sem=p_recv.at[w, hop],
            device_id={"src": partner}, device_id_type=MESH)
        return send, take

    def across_rest(whose):
        part = gather.at[whose, rest]
        return pltpu.make_async_remote_copy(
            src_ref=part, dst_ref=part, send_sem=b_send, recv_sem=b_recv,
            device_id={"src": partner}, device_id_type=MESH)

    def exists(at):
        return jnp.logical_and(at >= 0, at < lines)

    def each_link(k, hop, act):
        for w, way in enumerate(ways):
            origin = line - way * hop
            pl.when(jnp.logical_and(exists(origin), exists(line + way)))(
                lambda w=w, origin=origin: act(link(k, w, hop, origin)))

    def take_link(k, hop):
        for w, way in enumerate(ways):
            origin = line - way * (hop + 1)
            pl.when(exists(origin))(lambda w=w, origin=origin: link(k, w, hop, origin).wait_recv())

    def each_across(hop, act):
        for w, way in enumerate(ways):
            origin = line - way * (hop + 1)
            pl.when(exists(origin))(lambda w=w, origin=origin: act(*across(w, hop + 1, origin)))

    start = lambda copy: copy.start()

    def begin():
        own.wait()
        for copy in swaps:
            copy.wait()
        for s in range(STEPS):
            gather[me, s] = swap[owners[s]]
        across_rest(me).start()
        each_link(0, 0, start)
        across(0, 0, line)[0].start()
        each_link(1, 0, start)

    def along_most(hop):
        if hop == 0:
            across_rest(partner).wait_recv()
            each_link(2, 0, start)
        take_link(0, hop)
        if hop + 1 < lines - 1:
            each_link(0, hop + 1, start)
        each_across(hop, lambda send, take: send.start())

    def along_rest(hop):
        for k in (1, 2):
            take_link(k, hop)
            if hop + 1 < lines - 1:
                each_link(k, hop + 1, start)

    def finish():
        across_rest(me).wait_send()
        across(0, 0, line)[0].wait_send()
        for hop in range(lines - 1):
            for k in range(3):
                each_link(k, hop, lambda copy: copy.wait_send())
            each_across(hop, lambda send, take: send.wait_send())

    pumps = [begin]
    for hop in range(lines - 1):
        pumps.append(functools.partial(along_most, hop))
        pumps.append(functools.partial(along_rest, hop))

    def phase(row, t, takes, gives):
        over(row, t, 2, nx - 2)
        takes[0].wait_recv()
        over(row, t, near_rows, near_rows + 2)
        if gives:
            gives[0].start()
        pl.when(has_far)(lambda: takes[1].wait_recv())
        over(row, t, far_rows, far_rows + 2)
        if gives:
            pl.when(has_far)(lambda: gives[1].start())

    for t in range(STEPS):
        phase(velocity_row, t, s_halos[t], v_halos[t])
        if 0 < t < STEPS - 1:
            pumps.pop(0)()
        if t + 1 < STEPS:
            phase(stress_row, t, v_halos[t], s_halos[t + 1])
            pumps.pop(0)()
        else:
            phase(stress_row, t, v_halos[t], None)

    stores = []
    for src, dst in (
        (sig.at[STEPS, XX:XZ, inside[0], inside[1]], out_wave.at[3:4]),
        (sig.at[STEPS, XZ:YY, inside[0], inside[1]], out_wave.at[7:9]),
        (sig.at[STEPS, YY:, inside[0], inside[1]], out_wave.at[4:7]),
        (vel.at[STEPS, :, inside[0], inside[1]], out_wave.at[0:3]),
    ):
        stores.append(pltpu.make_async_copy(src, dst, store_sem.at[len(stores)]))
        stores[-1].start()


    per_row = ny // chunk

    def correlate(i, carry):
        for part in range(per_row):
            y = part * chunk
            j = i * per_row + part
            lam = mat[0, i, y:y + chunk, :]
            mu = mat[1, i, y:y + chunk, :]
            stiff = 1.0 / (3.0 * lam + 2.0 * mu)
            soft = DT / mu
            k_lam = jnp.zeros(lam.shape, jnp.float32)
            k_mu = jnp.zeros(lam.shape, jnp.float32)
            for t in range(STEPS):
                s = [sig[t + 1, c, i + 2, PAD + y:PAD + y + chunk, :] for c in range(6)]
                r = [gather[j, t, BANK[c]].astype(jnp.float32) for c in range(6)]
                theta = (s[XX] + s[YY] + s[ZZ]) * stiff
                trace = theta * (r[XX] + r[YY] + r[ZZ])
                k_lam = k_lam + trace
                k_mu = (k_mu + s[XX] * r[XX] + s[YY] * r[YY] + s[ZZ] * r[ZZ] - lam * trace
                        + 2.0 * (s[YZ] * r[YZ] + s[XZ] * r[XZ] + s[XY] * r[XY]))
            k_lam = DT * k_lam
            k_mu = soft * k_mu
            for z in range(chunk // rows):
                terms[y // rows + z, 0, i] = k_lam[z * rows:(z + 1) * rows]
                terms[y // rows + z, 1, i] = k_mu[z * rows:(z + 1) * rows]
        return carry

    group = nx // lines

    def sum_copy(d, g):
        peer = lax.rem(me + d, n)
        part = pl.ds(g * group, group)
        return pltpu.make_async_remote_copy(
            src_ref=terms.at[peer, :, part], dst_ref=arrived.at[me, :, part],
            send_sem=k_send.at[d, g], recv_sem=k_recv.at[d, g],
            device_id={"src": peer}, device_id_type=MESH)

    def add_group(g):
        lax.fori_loop(0, group, lambda i, carry: correlate(g * group + i, carry), 0)
        for d in range(1, n):
            sum_copy(d, g).start()

    across(0, 0, line)[1].wait_recv()
    add_group(line)
    for hop in range(lines - 1):
        while len(pumps) > 2 * (lines - 2 - hop):
            pumps.pop(0)()
        for w, way in enumerate(ways):
            origin = line - way * (hop + 1)

            def one(w=w, origin=origin):
                across(w, hop + 1, origin)[1].wait_recv()
                add_group(origin)

            pl.when(exists(origin))(one)
    finish()

    for pair in s_halos + v_halos:
        sent_halos(pair)
    arrived[me] = terms[me]
    for d in range(1, n):
        for g in range(lines):
            sum_copy(d, g).wait()
    for which, out in ((0, out_lam), (1, out_mu)):
        acc = arrived[0, which]
        for d in range(1, n):
            acc = acc + arrived[d, which]
        out[...] = acc
    for copy in stores:
        copy.wait()


def solution(mesh):
    n, m = mesh.shape["src"], mesh.shape["space"]

    def local(wavefield, strain_bank, owners, region, region_lambda, region_mu, region_buoyancy):
        nx, ny, nz = region.shape
        chunk = nx * ny // n
        rows = ny // n
        bank = strain_bank[0].reshape(6, n, chunk, nz)
        hbm = pl.BlockSpec(memory_space=pl.ANY)
        vmem = pl.BlockSpec(memory_space=pltpu.VMEM)
        smem = pl.BlockSpec(memory_space=pltpu.SMEM)
        dma = pltpu.SemaphoreType.DMA
        new, k_lam, k_mu = pl.pallas_call(
            functools.partial(kernel, n, m, nx, ny, chunk, 2),
            out_shape=(
                jax.ShapeDtypeStruct((9, nx, ny, nz), jnp.float32),
                jax.ShapeDtypeStruct((nx, rows, nz), jnp.float32),
                jax.ShapeDtypeStruct((nx, rows, nz), jnp.float32),
            ),
            in_specs=[smem, smem, smem, smem, vmem, hbm, hbm],
            out_specs=(hbm, vmem, vmem),
            scratch_shapes=[
                pltpu.VMEM((STEPS + 1, 3, nx + 4, ny + 2 * PAD, nz), jnp.float32),
                pltpu.VMEM((STEPS + 1, 6, nx + 4, ny + 2 * PAD, nz), jnp.float32),
                pltpu.VMEM((3, nx, ny, nz), jnp.float32),
                pltpu.VMEM((n, 6, chunk, nz), jnp.bfloat16),
                pltpu.VMEM((n, STEPS, 6, chunk, nz), jnp.bfloat16),
                pltpu.VMEM((n, 2, nx, rows, nz), jnp.float32),
                pltpu.VMEM((n, 2, nx, rows, nz), jnp.float32),
                dma((4,)), dma((4,)), dma,
                dma((n,)), dma((n,)), dma((3, 2, n // 2)), dma((3, 2, n // 2)),
                dma((2, n // 2)), dma((2, n // 2)), dma, dma, dma((n, n // 2)), dma((n, n // 2)),
                dma((STEPS + 1, 2)), dma((STEPS + 1, 2)), dma((STEPS + 1, 2)), dma((STEPS + 1, 2)),
            ],
            compiler_params=pltpu.CompilerParams(
                collective_id=0, has_side_effects=True, vmem_limit_bytes=56 * 1024 * 1024
            ),
        )(owners, region_lambda, region_mu, region_buoyancy, region, wavefield[0], bank)
        return new[None], k_lam, k_mu

    in_specs = (
        P("src", None, "space", None, None),
        P("src", None, "space", None, None),
        P(),
        P("space", None, None),
        P(),
        P(),
        P(),
    )
    out_specs = (
        P("src", None, "space", None, None),
        P("space", "src", None),
        P("space", "src", None),
    )
    return jax.shard_map(local, mesh=mesh, in_specs=in_specs, out_specs=out_specs, check_vma=False)
```

```python
import functools

import jax
import jax.numpy as jnp
from jax import lax
from jax.experimental import pallas as pl
from jax.experimental.pallas import tpu as pltpu
from jax.sharding import PartitionSpec as P

STEPS = 4
DT = 0.3
NEAR = 8.0 / 12.0
FAR = 1.0 / 12.0
MESH = pl.DeviceIdType.MESH

XX, XZ, XY, YY, ZZ, YZ = range(6)
BANK = (0, 4, 5, 1, 2, 3)
PAD = 8


def kernel(
    n, m, nx, ny, chunk, split,
    owners, t_lam, t_mu, t_buoy, region, wave, bank,
    out_wave, out_lam, out_mu,
    vel, sig, mat, swap, gather, terms, arrived,
    load_sem, store_sem, bank_sem,
    a2a_send, a2a_recv, c_send, c_recv, p_send, p_recv, b_send, b_recv, k_send, k_recv,
    vs_send, vs_recv, ss_send, ss_recv,
):
    me = lax.axis_index("src")
    pos = lax.axis_index("space")
    rows = ny // n
    first, last = pos == 0, pos == m - 1
    lower, upper = lax.rem(pos + m - 1, m), lax.rem(pos + 1, m)

    inside = (slice(2, 2 + nx), slice(PAD, PAD + ny))
    loads = []
    for src, dst in (
        (wave.at[3:4], sig.at[0, XX:XZ, inside[0], inside[1]]),
        (wave.at[7:9], sig.at[0, XZ:YY, inside[0], inside[1]]),
        (wave.at[4:7], sig.at[0, YY:, inside[0], inside[1]]),
        (wave.at[0:3], vel.at[0, :, inside[0], inside[1]]),
    ):
        loads.append(pltpu.make_async_copy(src, dst, load_sem.at[len(loads)]))
        loads[-1].start()
    own = pltpu.make_async_copy(bank.at[:, me], swap.at[me], bank_sem)
    own.start()

    barrier = pltpu.get_barrier_semaphore()
    for d in range(1, n):
        pl.semaphore_signal(barrier, inc=1, device_id={"src": lax.rem(me + d, n)}, device_id_type=MESH)
    for to in (lower, upper):
        pl.semaphore_signal(barrier, inc=1, device_id={"space": to}, device_id_type=MESH)
    pl.semaphore_wait(barrier, n - 1 + 2)

    swaps = []
    for d in range(1, n):
        peer = lax.rem(me + d, n)
        swaps.append(pltpu.make_async_remote_copy(
            src_ref=bank.at[:, peer], dst_ref=swap.at[me],
            send_sem=a2a_send.at[d], recv_sem=a2a_recv.at[d],
            device_id={"src": peer}, device_id_type=MESH))

    odd = lax.rem(pos, 2)
    has_far = jnp.where(odd == 1, pos, m - 1 - pos) < m - 1
    near_rows, far_rows = (1 - odd) * (nx - 2), odd * (nx - 2)

    def halos(buf, t, send, recv):
        near = pltpu.make_async_remote_copy(
            src_ref=buf.at[t, 0:3, pl.ds(near_rows + 2, 2), inside[1]],
            dst_ref=buf.at[t, 0:3, pl.ds(odd * (nx + 2), 2), inside[1]],
            send_sem=send.at[t, 0], recv_sem=recv.at[t, 0],
            device_id={"space": pos + 1 - 2 * odd}, device_id_type=MESH)
        far = pltpu.make_async_remote_copy(
            src_ref=buf.at[t, 0:3, pl.ds(far_rows + 2, 2), inside[1]],
            dst_ref=buf.at[t, 0:3, pl.ds((1 - odd) * (nx + 2), 2), inside[1]],
            send_sem=send.at[t, 1], recv_sem=recv.at[t, 1],
            device_id={"space": lax.rem(pos + m - 1 + 2 * odd, m)}, device_id_type=MESH)
        return near, far

    def sent_halos(pair):
        pair[0].wait_send()
        pl.when(has_far)(lambda: pair[1].wait_send())

    s_halos = [halos(sig, t, ss_send, ss_recv) for t in range(STEPS)]
    v_halos = [halos(vel, t, vs_send, vs_recv) for t in range(1, STEPS + 1)]

    for copy in loads[:2]:
        copy.wait()
    s_halos[0][0].start()
    pl.when(has_far)(lambda: s_halos[0][1].start())
    for copy in swaps:
        copy.start()

    wide = vel.shape[-1]
    for buf, times in ((sig, range(STEPS)), (vel, range(1, STEPS + 1))):
        for t in times:
            count = buf.shape[1]
            edge = jnp.zeros((count, nx, PAD, wide), jnp.float32)
            buf[t, :, 2:nx + 2, 0:PAD, :] = edge
            buf[t, :, 2:nx + 2, PAD + ny:, :] = edge

            @pl.when(first)
            def _():
                buf[t, 0:3, 0:2, PAD:PAD + ny, :] = jnp.zeros((3, 2, ny, wide), jnp.float32)

            @pl.when(last)
            def _():
                buf[t, 0:3, nx + 2:, PAD:PAD + ny, :] = jnp.zeros((3, 2, ny, wide), jnp.float32)

    def materials(i, carry):
        label = region[i]
        found = [jnp.zeros(label.shape, jnp.float32) for _ in range(3)]
        for which in range(t_lam.shape[0]):
            hit = label == which
            found = [jnp.where(hit, table[which], old)
                     for table, old in zip((t_lam, t_mu, t_buoy), found)]
        for which in range(3):
            mat[which, i] = found[which]
        return carry

    lax.fori_loop(0, nx, materials, 0)
    for copy in loads[2:]:
        copy.wait()

    tall = ny // split
    lane = lax.broadcasted_iota(jnp.int32, (tall, wide), 1)

    def deriv_x(buf, t, c, i, y):
        at = lambda k: buf[t, c, i + 2 + k, PAD + y:PAD + y + tall, :]
        return at(1) - at(-1), at(2) - at(-2)

    def deriv_y(buf, t, c, i, y):
        at = lambda k: buf[t, c, i + 2, PAD + y + k:PAD + y + k + tall, :]
        return at(1) - at(-1), at(2) - at(-2)

    def deriv_z(buf, t, c, i, y):
        f = buf[t, c, i + 2, PAD + y:PAD + y + tall, :]

        def at(k):
            moved = pltpu.roll(f, (-k) % wide, 1)
            keep = lane < wide - k if k > 0 else lane >= -k
            return jnp.where(keep, moved, 0.0)

        return at(1) - at(-1), at(2) - at(-2)

    def total(*pairs):
        near, far = pairs[0]
        for a, b in pairs[1:]:
            near, far = near + a, far + b
        return NEAR * near - FAR * far

    def velocity_row(t, i):
        for y in range(0, ny, tall):
            here = slice(PAD + y, PAD + y + tall)
            gain = DT * mat[2, i, y:y + tall, :]
            for c, (a, b, d) in enumerate(((XX, XY, XZ), (XY, YY, YZ), (XZ, YZ, ZZ))):
                force = total(deriv_x(sig, t, a, i, y), deriv_y(sig, t, b, i, y), deriv_z(sig, t, d, i, y))
                vel[t + 1, c, i + 2, here, :] = vel[t, c, i + 2, here, :] + gain * force

    def stress_row(t, i):
        s = t + 1
        for y in range(0, ny, tall):
            here = slice(PAD + y, PAD + y + tall)
            lam = DT * mat[0, i, y:y + tall, :]
            mu = DT * mat[1, i, y:y + tall, :]

            def put(c, change):
                sig[s, c, i + 2, here, :] = sig[t, c, i + 2, here, :] + change

            gx = total(deriv_x(vel, s, 0, i, y))
            gy = total(deriv_y(vel, s, 1, i, y))
            gz = total(deriv_z(vel, s, 2, i, y))
            div = lam * (gx + gy + gz)
            put(XX, div + 2.0 * mu * gx)
            put(YY, div + 2.0 * mu * gy)
            put(ZZ, div + 2.0 * mu * gz)
            put(YZ, mu * total(deriv_z(vel, s, 1, i, y), deriv_y(vel, s, 2, i, y)))
            put(XZ, mu * total(deriv_z(vel, s, 0, i, y), deriv_x(vel, s, 2, i, y)))
            put(XY, mu * total(deriv_y(vel, s, 0, i, y), deriv_x(vel, s, 1, i, y)))

    def over(row, t, start, stop):
        def body(i, carry):
            row(t, start + i)
            return carry
        lax.fori_loop(0, nx - 4 if isinstance(start, int) else 2, body, 0)

    line, side = me // 2, lax.rem(me, 2)
    lines = n // 2
    partner = me + 1 - 2 * side
    ways = (1, -1)
    most, rest = pl.ds(0, STEPS - 1), pl.ds(STEPS - 1, 1)
    items = ((most, False), (rest, False), (rest, True))

    def place(origin, swapped):
        return origin * 2 + (1 - side if swapped else side)

    def link(k, w, hop, origin):
        slots, swapped = items[k]
        part = gather.at[place(origin, swapped), slots]
        return pltpu.make_async_remote_copy(
            src_ref=part, dst_ref=part,
            send_sem=c_send.at[k, w, hop], recv_sem=c_recv.at[k, w, hop],
            device_id={"src": me + 2 * ways[w]}, device_id_type=MESH)

    def across(w, hop, origin):
        part = gather.at[place(origin, False), most]
        other = gather.at[place(origin, True), most]
        send = pltpu.make_async_remote_copy(
            src_ref=part, dst_ref=part, send_sem=p_send.at[w, hop], recv_sem=p_recv.at[w, hop],
            device_id={"src": partner}, device_id_type=MESH)
        take = pltpu.make_async_remote_copy(
            src_ref=other, dst_ref=other, send_sem=p_send.at[w, hop], recv_sem=p_recv.at[w, hop],
            device_id={"src": partner}, device_id_type=MESH)
        return send, take

    def across_rest(whose):
        part = gather.at[whose, rest]
        return pltpu.make_async_remote_copy(
            src_ref=part, dst_ref=part, send_sem=b_send, recv_sem=b_recv,
            device_id={"src": partner}, device_id_type=MESH)

    def exists(at):
        return jnp.logical_and(at >= 0, at < lines)

    def each_link(k, hop, act):
        for w, way in enumerate(ways):
            origin = line - way * hop
            pl.when(jnp.logical_and(exists(origin), exists(line + way)))(
                lambda w=w, origin=origin: act(link(k, w, hop, origin)))

    def take_link(k, hop):
        for w, way in enumerate(ways):
            origin = line - way * (hop + 1)
            pl.when(exists(origin))(lambda w=w, origin=origin: link(k, w, hop, origin).wait_recv())

    def each_across(hop, act):
        for w, way in enumerate(ways):
            origin = line - way * (hop + 1)
            pl.when(exists(origin))(lambda w=w, origin=origin: act(*across(w, hop + 1, origin)))

    start = lambda copy: copy.start()

    def begin():
        own.wait()
        for copy in swaps:
            copy.wait()
        for s in range(STEPS):
            gather[me, s] = swap[owners[s]]
        across_rest(me).start()
        each_link(0, 0, start)
        across(0, 0, line)[0].start()
        each_link(1, 0, start)

    def along_most(hop):
        if hop == 0:
            across_rest(partner).wait_recv()
            each_link(2, 0, start)
        take_link(0, hop)
        if hop + 1 < lines - 1:
            each_link(0, hop + 1, start)
        each_across(hop, lambda send, take: send.start())

    def along_rest(hop):
        for k in (1, 2):
            take_link(k, hop)
            if hop + 1 < lines - 1:
                each_link(k, hop + 1, start)

    def finish():
        across_rest(me).wait_send()
        across(0, 0, line)[0].wait_send()
        for hop in range(lines - 1):
            for k in range(3):
                each_link(k, hop, lambda copy: copy.wait_send())
            each_across(hop, lambda send, take: send.wait_send())

    pumps = [begin]
    for hop in range(lines - 1):
        pumps.append(functools.partial(along_most, hop))
        pumps.append(functools.partial(along_rest, hop))

    def phase(row, t, takes, gives):
        over(row, t, 2, nx - 2)
        takes[0].wait_recv()
        over(row, t, near_rows, near_rows + 2)
        if gives:
            gives[0].start()
        pl.when(has_far)(lambda: takes[1].wait_recv())
        over(row, t, far_rows, far_rows + 2)
        if gives:
            pl.when(has_far)(lambda: gives[1].start())

    for t in range(STEPS):
        phase(velocity_row, t, s_halos[t], v_halos[t])
        if t < STEPS - 1:
            pumps.pop(0)()
        if t + 1 < STEPS:
            phase(stress_row, t, v_halos[t], s_halos[t + 1])
            pumps.pop(0)()
        else:
            phase(stress_row, t, v_halos[t], None)

    stores = []
    for src, dst in (
        (sig.at[STEPS, XX:XZ, inside[0], inside[1]], out_wave.at[3:4]),
        (sig.at[STEPS, XZ:YY, inside[0], inside[1]], out_wave.at[7:9]),
        (sig.at[STEPS, YY:, inside[0], inside[1]], out_wave.at[4:7]),
        (vel.at[STEPS, :, inside[0], inside[1]], out_wave.at[0:3]),
    ):
        stores.append(pltpu.make_async_copy(src, dst, store_sem.at[len(stores)]))
        stores[-1].start()


    per_row = ny // chunk

    def correlate(i, carry):
        for part in range(per_row):
            y = part * chunk
            j = i * per_row + part
            lam = mat[0, i, y:y + chunk, :]
            mu = mat[1, i, y:y + chunk, :]
            stiff = 1.0 / (3.0 * lam + 2.0 * mu)
            soft = DT / mu
            k_lam = jnp.zeros(lam.shape, jnp.float32)
            k_mu = jnp.zeros(lam.shape, jnp.float32)
            for t in range(STEPS):
                s = [sig[t + 1, c, i + 2, PAD + y:PAD + y + chunk, :] for c in range(6)]
                r = [gather[j, t, BANK[c]].astype(jnp.float32) for c in range(6)]
                theta = (s[XX] + s[YY] + s[ZZ]) * stiff
                trace = theta * (r[XX] + r[YY] + r[ZZ])
                k_lam = k_lam + trace
                k_mu = (k_mu + s[XX] * r[XX] + s[YY] * r[YY] + s[ZZ] * r[ZZ] - lam * trace
                        + 2.0 * (s[YZ] * r[YZ] + s[XZ] * r[XZ] + s[XY] * r[XY]))
            k_lam = DT * k_lam
            k_mu = soft * k_mu
            for z in range(chunk // rows):
                terms[y // rows + z, 0, i] = k_lam[z * rows:(z + 1) * rows]
                terms[y // rows + z, 1, i] = k_mu[z * rows:(z + 1) * rows]
        return carry

    group = nx // lines

    def sum_copy(d, g):
        peer = lax.rem(me + d, n)
        part = pl.ds(g * group, group)
        return pltpu.make_async_remote_copy(
            src_ref=terms.at[peer, :, part], dst_ref=arrived.at[me, :, part],
            send_sem=k_send.at[d, g], recv_sem=k_recv.at[d, g],
            device_id={"src": peer}, device_id_type=MESH)

    def add_group(g):
        lax.fori_loop(0, group, lambda i, carry: correlate(g * group + i, carry), 0)
        for d in range(1, n):
            sum_copy(d, g).start()

    across(0, 0, line)[1].wait_recv()
    add_group(line)
    for hop in range(lines - 1):
        while len(pumps) > 2 * (lines - 2 - hop):
            pumps.pop(0)()
        for w, way in enumerate(ways):
            origin = line - way * (hop + 1)

            def one(w=w, origin=origin):
                across(w, hop + 1, origin)[1].wait_recv()
                add_group(origin)

            pl.when(exists(origin))(one)
    finish()

    for pair in s_halos + v_halos:
        sent_halos(pair)
    arrived[me] = terms[me]
    for d in range(1, n):
        for g in range(lines):
            sum_copy(d, g).wait()
    for which, out in ((0, out_lam), (1, out_mu)):
        acc = arrived[0, which]
        for d in range(1, n):
            acc = acc + arrived[d, which]
        out[...] = acc
    for copy in stores:
        copy.wait()


def solution(mesh):
    n, m = mesh.shape["src"], mesh.shape["space"]

    def local(wavefield, strain_bank, owners, region, region_lambda, region_mu, region_buoyancy):
        nx, ny, nz = region.shape
        chunk = nx * ny // n
        rows = ny // n
        bank = strain_bank[0].reshape(6, n, chunk, nz)
        hbm = pl.BlockSpec(memory_space=pl.ANY)
        vmem = pl.BlockSpec(memory_space=pltpu.VMEM)
        smem = pl.BlockSpec(memory_space=pltpu.SMEM)
        dma = pltpu.SemaphoreType.DMA
        new, k_lam, k_mu = pl.pallas_call(
            functools.partial(kernel, n, m, nx, ny, chunk, 2),
            out_shape=(
                jax.ShapeDtypeStruct((9, nx, ny, nz), jnp.float32),
                jax.ShapeDtypeStruct((nx, rows, nz), jnp.float32),
                jax.ShapeDtypeStruct((nx, rows, nz), jnp.float32),
            ),
            in_specs=[smem, smem, smem, smem, vmem, hbm, hbm],
            out_specs=(hbm, vmem, vmem),
            scratch_shapes=[
                pltpu.VMEM((STEPS + 1, 3, nx + 4, ny + 2 * PAD, nz), jnp.float32),
                pltpu.VMEM((STEPS + 1, 6, nx + 4, ny + 2 * PAD, nz), jnp.float32),
                pltpu.VMEM((3, nx, ny, nz), jnp.float32),
                pltpu.VMEM((n, 6, chunk, nz), jnp.bfloat16),
                pltpu.VMEM((n, STEPS, 6, chunk, nz), jnp.bfloat16),
                pltpu.VMEM((n, 2, nx, rows, nz), jnp.float32),
                pltpu.VMEM((n, 2, nx, rows, nz), jnp.float32),
                dma((4,)), dma((4,)), dma,
                dma((n,)), dma((n,)), dma((3, 2, n // 2)), dma((3, 2, n // 2)),
                dma((2, n // 2)), dma((2, n // 2)), dma, dma, dma((n, n // 2)), dma((n, n // 2)),
                dma((STEPS + 1, 2)), dma((STEPS + 1, 2)), dma((STEPS + 1, 2)), dma((STEPS + 1, 2)),
            ],
            compiler_params=pltpu.CompilerParams(
                collective_id=0, has_side_effects=True, vmem_limit_bytes=56 * 1024 * 1024
            ),
        )(owners, region_lambda, region_mu, region_buoyancy, region, wavefield[0], bank)
        return new[None], k_lam, k_mu

    in_specs = (
        P("src", None, "space", None, None),
        P("src", None, "space", None, None),
        P(),
        P("space", None, None),
        P(),
        P(),
        P(),
    )
    out_specs = (
        P("src", None, "space", None, None),
        P("space", "src", None),
        P("space", "src", None),
    )
    return jax.shard_map(local, mesh=mesh, in_specs=in_specs, out_specs=out_specs, check_vma=False)
```
